1024 devices in a mesh: grp: 64 (over x, z), sp: 16 (over y, core).
Axes of the slice: x: 4, y: 8, z: 16, core: 2. Of those that a mesh axis runs over, the one named last changes fastest.
Arguments:
- vis_feats: bfloat16 [16384, 1152], P('grp'), may hold values from -6 to 6
- proj_w: bfloat16 [1152, 4096], P(None, 'sp'), may hold values from -0.1875 to 0.1875
- text_embed: bfloat16 [262144, 4096], P('grp', 'sp'), may hold values from -6 to 6
- dest_group: int32 [16384], replicated, may hold values from 0 to 63, as said below
- layout: int32 [64, 4096], P('grp'), may hold values from 0 to 4095, each once within a row
- norm_gain: float32 [4096], P('sp'), may hold values from 0.1 to 1.9
- key_w: bfloat16 [4096, 512], P('sp'), may hold values from -0.09375 to 0.09375
- value_w: bfloat16 [4096, 512], P('sp'), may hold values from -0.09375 to 0.09375
Outputs:
- key_out: bfloat16 [262144, 512], P(('grp', 'sp'))
- value_out: bfloat16 [262144, 512], P(('grp', 'sp'))
The draws below stay inside these ranges and needn't reach their ends.
Inputs may be any that keep to these rules, and one draw needn't show every extreme that they name: `dest_group`: each block of 256 rows (one encoder shard's tokens) is 32 runs of 8 consecutive rows; a run names one group, and the runs of one block name distinct groups.
All inputs are finite; a program needn't handle non-finite values.
Results may differ from the reference program's by a relative error of at most 0.024.
Values may be sent and summed in bfloat16 or wider, within the bound.
No kernel may reach another device: no remote copies, remote signals or barrier semaphores. Data moves between devices by JAX's collectives and lax.ppermute only.
A program may use at most 32 MiB of HBM per device.

```python
import jax
import jax.numpy as jnp
from jax import lax

D = 4096
VW = 1152
KVW = 512
SEQ = 4096
NV = 16384
RUNS = 32
CAP = 8
N_GRP = 64
N_SP = 16


def draw_dest_group(key, part):
    shard_keys = jax.random.split(key, N_GRP)

    def one_shard(shard_key):
        return jax.random.permutation(shard_key, N_GRP)[:RUNS]
    run_groups = jax.vmap(one_shard)(shard_keys)
    return jnp.repeat(run_groups, CAP, axis=1).reshape(-1).astype(jnp.int32)


def block_levels(stream_key, dims, cuts, smallest, top_value):
    level, own = 1.0, jax.random.fold_in(stream_key, 6)
    for position, shards_of in cuts:
        steps = jnp.exp(jax.random.uniform(jax.random.fold_in(own, position), (shards_of,), jnp.float32, smallest / len(cuts), top_value / len(cuts)))
        level = level * jnp.repeat(steps, dims[position] // shards_of).reshape([-1 if axis == position else 1 for axis in range(len(dims))])
    return level


def centred(key, extent, width, bound, shards=(), kind=jnp.bfloat16):
    values = width * jax.random.normal(key, extent, jnp.float32)
    if shards:
        values = values * block_levels(key, extent, shards, -0.22, 0.18)
    return jnp.clip(values, -bound, bound).astype(kind)


def setup_inputs(seed: int = 0) -> dict:
    streams_of = jax.random.split(jax.random.key(seed), 9)
    return {
        "vis_feats": centred(streams_of[0], (NV, VW), 1.0, 6.0, ((0, 64),)),
        "proj_w": centred(streams_of[1], (VW, D), VW ** -0.5, 0.1875, ((1, 16),)),
        "text_embed": centred(streams_of[2], (N_GRP * SEQ, D), 1.0, 6.0, ((0, 64), (1, 16))),
        "dest_group": draw_dest_group(jax.random.fold_in(streams_of[8], 71), 0),
        "layout": jax.vmap(lambda own: jax.random.permutation(own, SEQ))(jax.random.split(streams_of[4], N_GRP)).reshape((N_GRP, SEQ)).astype(jnp.int32),
        "norm_gain": jnp.clip(1.0 + 0.18 * jax.random.normal(streams_of[5], (D,), jnp.float32), 0.1, 1.9),
        "key_w": centred(streams_of[6], (D, KVW), D ** -0.5, 0.09375, ((0, 16),)),
        "value_w": centred(streams_of[7], (D, KVW), D ** -0.5, 0.09375, ((0, 16),)),
    }


def reference(vis_feats, proj_w, text_embed, dest_group, layout, norm_gain, key_w, value_w):
    vis_proj = jnp.dot(vis_feats, proj_w, preferred_element_type=jnp.float32).astype(jnp.bfloat16)
    width_local = D // N_SP
    kv_weight = jnp.concatenate([key_w, value_w], axis=1).reshape(N_SP, width_local, 2 * KVW).astype(jnp.float32)

    def per_group(grp_idx):
        to_group = dest_group == grp_idx
        slot_rank = jnp.cumsum(to_group.astype(jnp.int32)) - 1
        order_row = lax.dynamic_index_in_dim(layout, grp_idx, 0, keepdims=False)
        positions = jnp.where(to_group, order_row[jnp.clip(slot_rank, 0, SEQ - 1)], SEQ).astype(jnp.int32)
        sequence = lax.dynamic_slice_in_dim(text_embed, (grp_idx * SEQ).astype(jnp.int32), SEQ, 0)
        sequence = sequence.at[positions].set(vis_proj, mode='drop')
        sequence_f = sequence.astype(jnp.float32)
        mean_sq = lax.optimization_barrier(jnp.mean(sequence_f * sequence_f, axis=1))
        scaled = (sequence_f * norm_gain).astype(jnp.bfloat16)
        blocks = scaled.reshape(SEQ, N_SP, width_local).astype(jnp.float32)
        partials = jnp.einsum('sjd,jdc->jsc', blocks, kv_weight).astype(jnp.bfloat16)
        partials = lax.optimization_barrier(partials)
        key_value = lax.optimization_barrier(jnp.sum(partials.astype(jnp.float32), axis=0))
        inv_rms = lax.rsqrt(mean_sq + 1e-05)[:, None]
        key_part = (key_value[:, :KVW] * inv_rms).astype(jnp.bfloat16)
        value_part = (key_value[:, KVW:] * inv_rms).astype(jnp.bfloat16)
        return (key_part, value_part)
    key_all, value_all = lax.map(per_group, jnp.arange(N_GRP, dtype=jnp.int32))
    return (key_all.reshape(N_GRP * SEQ, KVW), value_all.reshape(N_GRP * SEQ, KVW))
```

```python
import functools

import jax
import jax.numpy as jnp
from jax import lax
from jax.experimental import pallas as pl
from jax.experimental.pallas import tpu as pltpu
from jax.sharding import Mesh
from jax.sharding import PartitionSpec as P

D = 4096
LANES = 128
EXTRA = 16
EPS = 1e-05
F32 = jnp.float32
BF16 = jnp.bfloat16


def three_parts(x):
    hi = x.astype(BF16).astype(F32)
    rest = x - hi
    mid = rest.astype(BF16).astype(F32)
    low = (rest - mid).astype(BF16).astype(F32)
    return [hi, mid, low]


def source_kernel(capacity, n_y, feats_ref, proj_ref, weight_ref, squares_ref, out_ref):
    tokens = feats_ref.shape[0]
    half = tokens // 2
    per_core = capacity // 2
    projected = jnp.dot(feats_ref[...], proj_ref[...], preferred_element_type=F32).astype(BF16)
    row = lax.broadcasted_iota(jnp.int32, (tokens, tokens), 0)
    col = lax.broadcasted_iota(jnp.int32, (tokens, tokens), 1)
    core = (row >= half).astype(jnp.int32)
    inner = row - core * half
    run = lax.div(inner, per_core)
    token = run * capacity + core * per_core + (inner - run * per_core)
    order = (col == token).astype(F32).astype(BF16)
    tokens_by_core = jnp.dot(order, projected, preferred_element_type=F32)
    lane_squares = jnp.sum((tokens_by_core * tokens_by_core).T, axis=0, keepdims=True)
    products = jnp.dot(
        tokens_by_core.astype(BF16), weight_ref[...], preferred_element_type=F32
    ).astype(BF16)
    text_rows = squares_ref.shape[1]
    pad = jnp.zeros((EXTRA - 3 * (text_rows + 1), LANES), F32)
    for y in range(n_y):
        for c in range(2):
            to = 2 * y + c
            out_ref[to, :half, :] = products[c * half : (c + 1) * half, y * LANES : (y + 1) * LANES]
            parts = three_parts(squares_ref[to])
            parts += three_parts(lane_squares[:, c * half : (c + 1) * half])
            out_ref[to, half:, :] = jnp.concatenate(parts + [pad], axis=0).astype(BF16)


def route_kernel(text_rows, target_ref, parts_ref, out_ref, squares_ref):
    half = parts_ref.shape[1] - EXTRA
    sums = jnp.sum(parts_ref[:, :half, :].astype(F32), axis=0)
    extra = jnp.sum(parts_ref[:, half:, :].astype(F32), axis=0)
    text = extra[:text_rows] + extra[text_rows : 2 * text_rows] + extra[2 * text_rows : 3 * text_rows]
    squares_ref[...] = jnp.concatenate(
        [text, jnp.zeros((8 - text_rows, LANES), F32)], axis=0
    )
    first = 3 * text_rows
    visual = extra[first : first + 1] + extra[first + 1 : first + 2] + extra[first + 2 : first + 3]
    scale = jnp.broadcast_to(lax.rsqrt(visual / D + EPS), (half, half)).T
    rows = (sums * scale).astype(BF16)
    slot = lax.broadcasted_iota(jnp.int32, (out_ref.shape[0], half), 0)
    place = (slot == target_ref[0:1, :]).astype(F32).astype(BF16)
    out_ref[...] = jnp.dot(place, rows, preferred_element_type=F32).astype(BF16)


def finish_kernel(sums_ref, squares_ref, slots_ref, own_ref, other_ref, key_ref, value_ref):
    rows = sums_ref.shape[0]
    n_y, slots, _ = own_ref.shape
    position = lax.broadcasted_iota(jnp.int32, (rows, slots), 0)
    own_f = (position == slots_ref[0:1, :]).astype(F32)
    other_f = (position == slots_ref[1:2, :]).astype(F32)
    is_visual = jnp.sum(own_f + other_f, axis=1, keepdims=True) > 0.5
    own = own_f.astype(BF16)
    other = other_f.astype(BF16)
    inverse = lax.rsqrt(squares_ref[...] / D + EPS)
    scale = jnp.concatenate(
        [
            jnp.broadcast_to(inverse[i : i + 1, :], (LANES, LANES)).T
            for i in range(rows // LANES)
        ],
        axis=0,
    )
    for y in range(n_y):
        visual = jnp.dot(own, own_ref[y], preferred_element_type=F32)
        visual += jnp.dot(other, other_ref[y], preferred_element_type=F32)
        text = sums_ref[:, y * LANES : (y + 1) * LANES].astype(F32) * scale
        block = jnp.where(is_visual, visual, text).astype(BF16)
        if y < n_y // 2:
            key_ref[:, y * LANES : (y + 1) * LANES] = block
        else:
            z = y - n_y // 2
            value_ref[:, z * LANES : (z + 1) * LANES] = block


def vmem(n):
    return [pl.BlockSpec(memory_space=pltpu.VMEM)] * n


PARAMS = pltpu.CompilerParams(vmem_limit_bytes=24 * 2**20)


def local(vis_feats, proj_w, text_embed, dest_group, layout, norm_gain, key_w, value_w):
    n_grp = lax.axis_size("grp")
    n_y = lax.axis_size("y")
    n_sp = 2 * n_y
    h = lax.axis_index("grp")
    c = lax.axis_index("core")
    s = lax.axis_index("y") * 2 + c
    seq_len = text_embed.shape[0]
    rows_here = seq_len // n_sp
    tokens = vis_feats.shape[0]
    run_count = n_grp // 2
    capacity = tokens // run_count
    per_core = capacity // 2
    half = tokens // 2
    columns = key_w.shape[1] + value_w.shape[1]
    text_rows = rows_here // LANES

    weight = jnp.concatenate([key_w, value_w], axis=1).astype(F32) * norm_gain[:, None]
    weight = weight.astype(BF16)
    text_sums = lax.psum_scatter(
        jnp.dot(text_embed, weight, preferred_element_type=F32).astype(BF16),
        ("y", "core"),
        scatter_dimension=0,
        tiled=True,
    )
    text_f = text_embed.astype(F32)
    squares = jnp.sum(text_f * text_f, axis=1).reshape(n_sp, text_rows, LANES)

    outgoing = pl.pallas_call(
        functools.partial(source_kernel, capacity, n_y),
        out_shape=jax.ShapeDtypeStruct((n_sp, half + EXTRA, LANES), BF16),
        in_specs=vmem(4),
        out_specs=pl.BlockSpec(memory_space=pltpu.VMEM),
        compiler_params=PARAMS,
        name="source",
    )(vis_feats, proj_w, weight, squares)
    parts = lax.all_to_all(outgoing, ("y", "core"), 0, 0, tiled=True)

    run_heads = dest_group.reshape(n_grp, run_count, capacity)[:, :, 0]
    own_runs = lax.dynamic_index_in_dim(run_heads, h, 0, keepdims=False)
    target = own_runs[:, None] * per_core + jnp.arange(per_core, dtype=jnp.int32)[None, :]
    target = jnp.broadcast_to(target.reshape(1, half), (8, half))
    routed, my_squares = pl.pallas_call(
        functools.partial(route_kernel, text_rows),
        out_shape=(
            jax.ShapeDtypeStruct((n_grp * per_core, LANES), BF16),
            jax.ShapeDtypeStruct((8, LANES), F32),
        ),
        in_specs=vmem(2),
        out_specs=tuple(vmem(2)),
        compiler_params=PARAMS,
        name="route",
    )(target, parts)
    arrived = lax.all_to_all(
        routed.reshape(n_grp, per_core, LANES), "grp", 0, 0, tiled=True
    ).reshape(n_grp * per_core, LANES)
    own = lax.all_to_all(
        jnp.broadcast_to(arrived[None], (n_y, n_grp * per_core, LANES)), "y", 0, 0, tiled=True
    )
    other = lax.ppermute(own, "core", [(0, 1), (1, 0)])

    senders = jnp.any(run_heads == h, axis=1)
    group = jnp.arange(n_grp, dtype=jnp.int32)
    earlier = jnp.sum(
        jnp.where(senders[None, :] & (group[None, :] < group[:, None]), 1, 0), axis=1
    )
    first_ranks = layout[0, : n_grp * capacity].reshape(n_grp, capacity)
    where = jnp.sum(
        jnp.where((earlier[:, None] == group[None, :])[:, :, None], first_ranks[None], 0), axis=1
    )
    where = jnp.where(senders[:, None], where - s * rows_here, -1)
    where = where.reshape(n_grp, 2, per_core).transpose(1, 0, 2).reshape(2, n_grp * per_core)
    mine = lax.dynamic_index_in_dim(where, c, 0)
    theirs = lax.dynamic_index_in_dim(where, 1 - c, 0)
    slots = jnp.concatenate([mine, theirs, jnp.full((6, n_grp * per_core), -1, jnp.int32)], axis=0)

    return pl.pallas_call(
        finish_kernel,
        out_shape=(
            jax.ShapeDtypeStruct((rows_here, key_w.shape[1]), BF16),
            jax.ShapeDtypeStruct((rows_here, value_w.shape[1]), BF16),
        ),
        in_specs=vmem(5),
        out_specs=tuple(vmem(2)),
        compiler_params=PARAMS,
        name="finish",
    )(text_sums, my_squares, slots, own, other)


def solution(mesh):
    n_grp, n_sp = mesh.devices.shape
    split = Mesh(mesh.devices.reshape(n_grp, n_sp // 2, 2), ("grp", "y", "core"))
    sp = ("y", "core")
    return jax.shard_map(
        local,
        mesh=split,
        in_specs=(
            P("grp", None),
            P(None, sp),
            P("grp", sp),
            P(),
            P("grp", None),
            P(sp),
            P(sp, None),
            P(sp, None),
        ),
        out_specs=(P(("grp", "y", "core"), None), P(("grp", "y", "core"), None)),
        check_vma=False,
    )
```

```python
import functools

import jax
import jax.numpy as jnp
from jax import lax
from jax.experimental import pallas as pl
from jax.experimental.pallas import tpu as pltpu
from jax.sharding import Mesh
from jax.sharding import PartitionSpec as P

D = 4096
LANES = 128
STRIPE = 16
EPS = 1e-05
F32 = jnp.float32
BF16 = jnp.bfloat16
PARAMS = pltpu.CompilerParams(vmem_limit_bytes=32 * 2**20)


def vmem(n):
    return [pl.BlockSpec(memory_space=pltpu.VMEM)] * n


def one_hot(mask):
    return mask.astype(F32).astype(BF16)


def dot(a, b):
    return jnp.dot(a, b, preferred_element_type=F32)


def three_parts(x):
    hi = x.astype(BF16).astype(F32)
    rest = x - hi
    mid = rest.astype(BF16).astype(F32)
    low = (rest - mid).astype(BF16).astype(F32)
    return [hi, mid, low]


def source_kernel(target_ref, feats_ref, proj_ref, out_ref):
    projected = dot(feats_ref[...], proj_ref[...]).astype(BF16)
    slot = lax.broadcasted_iota(jnp.int32, (out_ref.shape[0], feats_ref.shape[0]), 0)
    place = one_hot(slot == target_ref[0:1, :])
    out_ref[...] = dot(place, projected).astype(BF16)


def source(target, feats, proj, slots):
    return pl.pallas_call(
        source_kernel,
        out_shape=jax.ShapeDtypeStruct((slots, proj.shape[1]), BF16),
        in_specs=vmem(3),
        out_specs=pl.BlockSpec(memory_space=pltpu.VMEM),
        compiler_params=PARAMS,
        name="source",
    )(target, feats, proj)


def copy_kernel(order_ref, block_ref, out_ref):
    out_ref[...] = block_ref[...]


def pick(order, blocks):
    n = order.shape[0]
    spec = (1,) + blocks.shape[1:]
    return pl.pallas_call(
        copy_kernel,
        out_shape=jax.ShapeDtypeStruct((n,) + blocks.shape[1:], blocks.dtype),
        grid_spec=pltpu.PrefetchScalarGridSpec(
            num_scalar_prefetch=1,
            grid=(n,),
            in_specs=[pl.BlockSpec(spec, lambda i, order: (order[i], 0, 0))],
            out_specs=pl.BlockSpec(spec, lambda i, order: (i, 0, 0)),
        ),
        compiler_params=PARAMS,
        name="pick",
    )(order, blocks)


def product_kernel(
    first, order_ref, own_ref, other_ref, w_own_ref, w_other_ref, v_own_ref, v_other_ref,
    slots_ref, out_ref, squares_ref,
):
    rows = own_ref.shape[1]
    block = order_ref[first + pl.program_id(0)]
    position = lax.broadcasted_iota(jnp.int32, (rows, slots_ref.shape[1]), 0) + block * rows
    hit = (position == slots_ref[0:1, :]).astype(F32)
    is_visual = jnp.sum(hit, axis=1, keepdims=True) > 0.5
    hit = hit.astype(BF16)
    ones = jnp.ones((8, own_ref.shape[2]), BF16)
    total = None
    lane_squares = None
    for text, visual, weight in (
        (own_ref, v_own_ref, w_own_ref),
        (other_ref, v_other_ref, w_other_ref),
    ):
        x = jnp.where(is_visual, dot(hit, visual[...]), text[0].astype(F32))
        term = dot(x.astype(BF16), weight[...])
        total = term if total is None else total + term
        square = x * x
        hi = square.astype(BF16)
        low = (square - hi.astype(F32)).astype(BF16)
        for part in (hi, low):
            term = lax.dot_general(
                ones, part, (((1,), (1,)), ((), ())), preferred_element_type=F32
            )
            lane_squares = term if lane_squares is None else lane_squares + term
    out_ref[0] = total.astype(BF16)
    squares_ref[0] = lane_squares


def products(order, first, count, own, other, w_own, w_other, v_own, v_other, slots):
    _, rows, feats = own.shape
    cols = w_own.shape[1]
    whole = lambda a: pl.BlockSpec(a.shape, lambda i, order: (0,) * a.ndim)
    return pl.pallas_call(
        functools.partial(product_kernel, first),
        out_shape=(
            jax.ShapeDtypeStruct((count, rows, cols), BF16),
            jax.ShapeDtypeStruct((count, 8, rows), F32),
        ),
        grid_spec=pltpu.PrefetchScalarGridSpec(
            num_scalar_prefetch=1,
            grid=(count,),
            in_specs=[
                pl.BlockSpec((1, rows, feats), lambda i, order: (order[first + i], 0, 0)),
                pl.BlockSpec((1, rows, feats), lambda i, order: (first + i, 0, 0)),
                whole(w_own),
                whole(w_other),
                whole(v_own),
                whole(v_other),
                whole(slots),
            ],
            out_specs=(
                pl.BlockSpec((1, rows, cols), lambda i, order: (i, 0, 0)),
                pl.BlockSpec((1, 8, rows), lambda i, order: (i, 0, 0)),
            ),
        ),
        compiler_params=PARAMS,
        cost_estimate=pl.CostEstimate(
            flops=count * 4 * rows * feats * (cols + slots.shape[1]),
            bytes_accessed=count * rows * (4 * feats + 2 * cols) + 8 * feats * cols,
            transcendentals=0,
        ),
        name="products",
    )(order, own, other, w_own, w_other, v_own, v_other, slots)


def stripe_of(squares, width):
    parts = three_parts(squares)
    pad = jnp.zeros((STRIPE - 3, squares.shape[1]), F32)
    stripe = jnp.concatenate(parts + [pad], axis=0)
    return stripe.astype(BF16)


def stripe_sum(stripe):
    return stripe[0:1] + stripe[1:2] + stripe[2:3]


def leaf_kernel(part, product_ref, squares_ref, out_ref):
    rows = product_ref.shape[1]
    out_ref[:rows, :] = product_ref[0]
    if part == 0:
        squares = squares_ref[0, 0:1, :]
        wide = jnp.concatenate([squares, jnp.zeros_like(squares)], axis=1)
        out_ref[rows:, :] = stripe_of(wide, out_ref.shape[1])


def hop_kernel(part, came_rows, product_ref, squares_ref, came_ref, out_ref):
    rows = product_ref.shape[1]
    for i in range(2):
        to = slice(i * rows, (i + 1) * rows)
        if i * rows < came_rows:
            total = product_ref[i].astype(F32) + came_ref[to, :].astype(F32)
            out_ref[to, :] = total.astype(BF16)
        else:
            out_ref[to, :] = product_ref[i]
    if part == 0:
        squares = jnp.concatenate([squares_ref[0, 0:1, :], squares_ref[1, 0:1, :]], axis=1)
        squares += stripe_sum(came_ref[came_rows:, :].astype(F32))
        out_ref[2 * rows :, :] = stripe_of(squares, out_ref.shape[1])


def add_call(kernel, name, part, at, count, product, squares, came, cols, rows_out):
    rows = product.shape[1]
    whole = lambda a: pl.BlockSpec(a.shape, lambda i: (0,) * a.ndim)
    return pl.pallas_call(
        kernel,
        out_shape=jax.ShapeDtypeStruct((rows_out, cols), BF16),
        grid=(1,),
        in_specs=[
            pl.BlockSpec((pl.Element(count), pl.Element(rows), pl.Element(cols)), lambda i: (at, 0, part * cols)),
            pl.BlockSpec((pl.Element(count), pl.Element(8), pl.Element(rows)), lambda i: (at, 0, 0)),
        ]
        + [whole(a) for a in came],
        out_specs=pl.BlockSpec((rows_out, cols), lambda i: (0, 0)),
        compiler_params=PARAMS,
        name=name,
    )(product, squares, *came)


def finish_kernel(product_ref, squares_ref, k_ref, v_ref, k2_ref, v2_ref, key_ref, value_ref):
    rows = product_ref.shape[1]
    cols = key_ref.shape[1]
    squares = squares_ref[0, 0:1, :]
    squares += stripe_sum(k_ref[2 * rows :, :].astype(F32))[:, :rows]
    squares += stripe_sum(k2_ref[rows:, :].astype(F32))[:, rows:]
    inverse = lax.rsqrt(squares / D + EPS)
    for i in range(rows // LANES):
        to = slice(i * LANES, (i + 1) * LANES)
        scale = jnp.broadcast_to(inverse[:, to], (LANES, LANES)).T
        for out_ref, a_ref, b_ref, at in (
            (key_ref, k_ref, k2_ref, 0),
            (value_ref, v_ref, v2_ref, cols),
        ):
            for j in range(cols // LANES):
                lane = slice(j * LANES, (j + 1) * LANES)
                own = product_ref[0, to, at + j * LANES : at + (j + 1) * LANES].astype(F32)
                total = own + a_ref[to, lane].astype(F32) + b_ref[to, lane].astype(F32)
                out_ref[to, lane] = (total * scale).astype(BF16)


def finish(product, squares, k, v, k2, v2, cols):
    rows = product.shape[1]
    whole = lambda a: pl.BlockSpec(a.shape, lambda i: (0,) * a.ndim)
    last = product.shape[0] - 1
    return pl.pallas_call(
        finish_kernel,
        out_shape=(jax.ShapeDtypeStruct((rows, cols), BF16),) * 2,
        grid=(1,),
        in_specs=[
            pl.BlockSpec((1,) + product.shape[1:], lambda i: (last, 0, 0)),
            pl.BlockSpec((1,) + squares.shape[1:], lambda i: (last, 0, 0)),
        ]
        + [whole(a) for a in (k, v, k2, v2)],
        out_specs=(pl.BlockSpec((rows, cols), lambda i: (0, 0)),) * 2,
        compiler_params=PARAMS,
        name="finish",
    )(product, squares, k, v, k2, v2)


def local(vis_feats, proj_w, text_embed, dest_group, layout, norm_gain, key_w, value_w):
    n_grp = lax.axis_size("grp")
    n_y = lax.axis_size("y")
    h = lax.axis_index("grp")
    y = lax.axis_index("y")
    c = lax.axis_index("core")
    seq_len, feats = text_embed.shape
    rows = seq_len // (2 * n_y)
    tokens = vis_feats.shape[0]
    run_count = n_grp // 2
    capacity = tokens // run_count
    slot_count = n_grp * capacity
    cols = key_w.shape[1]
    swap = [(0, 1), (1, 0)]
    ring = []
    for i in range(n_y):
        ring.append((2 * i, 2 * ((i + 1) % n_y)))
        ring.append((2 * i + 1, 2 * ((i - 1) % n_y) + 1))

    own_dest = lax.dynamic_slice_in_dim(dest_group, h * tokens, tokens, 0)
    target = own_dest * capacity + jnp.arange(tokens, dtype=jnp.int32) % capacity
    target = jnp.broadcast_to(target[None, :], (8, tokens))
    outgoing = source(target, vis_feats, proj_w, slot_count)
    arrived = lax.all_to_all(
        outgoing.reshape(n_grp, capacity, feats), "grp", 0, 0, tiled=True
    ).reshape(slot_count, feats)

    weight = jnp.concatenate([key_w, value_w], axis=1).astype(F32) * norm_gain[:, None]
    weight = weight.astype(BF16)
    w_other = lax.ppermute(weight, "core", swap)

    far = n_y // 2
    offset = [far] + [o for o in range(far - 1, 0, -1) for _ in (0, 1)] + [0]
    second = [0] + [0, 1] * (far - 1) + [0]
    offset = jnp.asarray(offset, jnp.int32)
    second = jnp.asarray(second, jnp.int32)
    up = 2 * ((y + offset) % n_y) + second
    down = 2 * ((y - offset + n_y) % n_y) + 1 - second
    mine = jnp.where(c == 0, up, down)
    theirs = jnp.where(c == 0, down, up)
    blocks = text_embed.reshape(2 * n_y, rows, feats)
    other = lax.ppermute(pick(theirs, blocks), "core", swap)

    run_heads = dest_group.reshape(n_grp, run_count, capacity)[:, :, 0]
    senders = jnp.any(run_heads == h, axis=1)
    group = jnp.arange(n_grp, dtype=jnp.int32)
    earlier = jnp.sum(
        jnp.where(senders[None, :] & (group[None, :] < group[:, None]), 1, 0), axis=1
    )
    first_ranks = layout[0, :slot_count].reshape(n_grp, capacity)
    where = jnp.sum(
        jnp.where((earlier[:, None] == group[None, :])[:, :, None], first_ranks[None], 0), axis=1
    )
    where = jnp.where(senders[:, None], where, -1)
    slots = jnp.broadcast_to(where.reshape(1, slot_count), (8, slot_count))

    arrived_other = lax.ppermute(arrived, "core", swap)
    operands = (blocks, other, weight, w_other, arrived, arrived_other, slots)
    leaf, leaf_squares = products(mine, 0, 1, *operands)
    product, squares = products(mine, 1, n_y - 1, *operands)

    flat = ("y", "core")
    streams = []
    for part in range(2):
        sent = add_call(
            functools.partial(leaf_kernel, part), "leaf", part, 0, 1, leaf, leaf_squares, [],
            cols, rows + (STRIPE if part == 0 else 0),
        )
        streams.append(lax.ppermute(sent, flat, ring))
    came_rows = rows
    for step in range(far - 1):
        for part in range(2):
            sent = add_call(
                functools.partial(hop_kernel, part, came_rows), "hop", part, 2 * step, 2,
                product, squares, [streams[part]], cols,
                2 * rows + (STRIPE if part == 0 else 0),
            )
            streams[part] = lax.ppermute(sent, flat, ring)
        came_rows = 2 * rows
    key_sums, value_sums = streams
    key_rest = lax.ppermute(key_sums[rows:], "core", swap)
    value_rest = lax.ppermute(value_sums[rows:], "core", swap)
    return finish(product, squares, key_sums, value_sums, key_rest, value_rest, cols)


def solution(mesh):
    n_grp, n_sp = mesh.devices.shape
    split = Mesh(mesh.devices.reshape(n_grp, n_sp // 2, 2), ("grp", "y", "core"))
    sp = ("y", "core")
    return jax.shard_map(
        local,
        mesh=split,
        in_specs=(
            P("grp", None),
            P(None, sp),
            P("grp", sp),
            P(),
            P("grp", None),
            P(sp),
            P(sp, None),
            P(sp, None),
        ),
        out_specs=(P(("grp", "y", "core"), None), P(("grp", "y", "core"), None)),
        check_vma=False,
    )
```

```python
import functools

import jax
import jax.numpy as jnp
from jax import lax
from jax.experimental import pallas as pl
from jax.experimental.pallas import tpu as pltpu
from jax.sharding import Mesh
from jax.sharding import PartitionSpec as P

D = 4096
LANES = 128
STRIPE = 16
EPS = 1e-05
F32 = jnp.float32
BF16 = jnp.bfloat16
PARAMS = pltpu.CompilerParams(vmem_limit_bytes=32 * 2**20)


def vmem(n):
    return [pl.BlockSpec(memory_space=pltpu.VMEM)] * n


def in_hbm(x):
    return pltpu.with_memory_space_constraint(x, pltpu.HBM)


def one_hot(mask):
    return mask.astype(F32).astype(BF16)


def dot(a, b):
    return jnp.dot(a, b, preferred_element_type=F32)


def three_parts(x):
    hi = x.astype(BF16).astype(F32)
    rest = x - hi
    mid = rest.astype(BF16).astype(F32)
    low = (rest - mid).astype(BF16).astype(F32)
    return [hi, mid, low]


def source_kernel(capacity, group_ref, dest_ref, feats_ref, proj_ref, out_ref, acc_ref):
    step = pl.program_id(0)
    lines = feats_ref.shape[0] // LANES

    @pl.when(step == 0)
    def _():
        acc_ref[...] = jnp.zeros_like(acc_ref)

    acc_ref[...] += dot(feats_ref[...], proj_ref[...])

    @pl.when(step == pl.num_programs(0) - 1)
    def _():
        first = lax.rem(group_ref[0] * lines, dest_ref.shape[0])
        lane = lax.broadcasted_iota(jnp.int32, (1, LANES), 1)
        slot = lax.broadcasted_iota(jnp.int32, (out_ref.shape[0], LANES), 0)
        total = None
        for i in range(lines):
            target = dest_ref[pl.ds(first + i, 1), :] * capacity + lax.rem(lane, capacity)
            rows = acc_ref[i * LANES : (i + 1) * LANES, :].astype(BF16)
            term = dot(one_hot(slot == target), rows)
            total = term if total is None else total + term
        out_ref[...] = total.astype(BF16)


def source(group, dest, feats, proj, slots, capacity):
    tokens, width = feats.shape
    cols = proj.shape[1]
    lines = tokens // LANES
    chunk = 384 if width % 384 == 0 else width
    return pl.pallas_call(
        functools.partial(source_kernel, capacity),
        out_shape=jax.ShapeDtypeStruct((slots, cols), BF16),
        grid_spec=pltpu.PrefetchScalarGridSpec(
            num_scalar_prefetch=1,
            grid=(width // chunk,),
            in_specs=[
                pl.BlockSpec((8, LANES), lambda i, group: (group[0] * lines // 8, 0)),
                pl.BlockSpec((tokens, chunk), lambda i, group: (0, i)),
                pl.BlockSpec((chunk, cols), lambda i, group: (i, 0)),
            ],
            out_specs=pl.BlockSpec((slots, cols), lambda i, group: (0, 0)),
            scratch_shapes=[pltpu.VMEM((tokens, cols), F32)],
        ),
        compiler_params=PARAMS,
        name="source",
    )(group, in_hbm(dest), in_hbm(feats), in_hbm(proj))


def slots_kernel(capacity, lines, group_ref, dest_ref, layout_ref, out_ref):
    slots = out_ref.shape[1]
    hits = one_hot(dest_ref[...] == group_ref[0])
    ones = jnp.ones((8, LANES), BF16)
    counts = lax.dot_general(
        ones, hits, (((1,), (1,)), ((), ())), preferred_element_type=F32
    ).astype(BF16)
    shape = (dest_ref.shape[0], slots)
    sender = lax.div(lax.broadcasted_iota(jnp.int32, shape, 0), lines)
    slot = lax.div(lax.broadcasted_iota(jnp.int32, shape, 1), capacity)
    before = dot(counts, one_hot(sender < slot)).astype(jnp.int32)
    sends = dot(counts, one_hot(sender == slot))
    token = lax.rem(lax.broadcasted_iota(jnp.int32, (1, slots), 1), capacity)
    rank = lax.broadcasted_iota(jnp.int32, (slots, slots), 0)
    chosen = one_hot(rank == before[0:1, :] + token)
    order = layout_ref[...]
    high = lax.div(order, 64)
    both = jnp.concatenate(
        [high.astype(F32), (order - high * 64).astype(F32), jnp.zeros((6, slots), F32)], axis=0
    )
    found = dot(both.astype(BF16), chosen).astype(jnp.int32)
    place = found[0:1, :] * 64 + found[1:2, :]
    place = jnp.where(sends[0:1, :] > 0.5, place, -1)
    out_ref[...] = jnp.broadcast_to(place, out_ref.shape)


def slot_positions(group, dest, layout, slots, capacity, lines):
    return pl.pallas_call(
        functools.partial(slots_kernel, capacity, lines),
        out_shape=jax.ShapeDtypeStruct((8, slots), jnp.int32),
        grid_spec=pltpu.PrefetchScalarGridSpec(
            num_scalar_prefetch=1,
            grid=(1,),
            in_specs=[
                pl.BlockSpec(dest.shape, lambda i, group: (0, 0)),
                pl.BlockSpec((1, slots), lambda i, group: (0, 0)),
            ],
            out_specs=pl.BlockSpec((8, slots), lambda i, group: (0, 0)),
        ),
        compiler_params=PARAMS,
        cost_estimate=pl.CostEstimate(flops=1, bytes_accessed=1, transcendentals=0),
        name="slots",
    )(group, dest, layout)


def lane_sums(x):
    square = x * x
    hi = square.astype(BF16)
    low = (square - hi.astype(F32)).astype(BF16)
    ones = jnp.ones((8, x.shape[1]), BF16)
    dims = (((1,), (1,)), ((), ()))
    total = lax.dot_general(ones, hi, dims, preferred_element_type=F32)
    return total + lax.dot_general(ones, low, dims, preferred_element_type=F32)


def text_kernel(order_ref, own_ref, other_ref, w_own_ref, w_other_ref, out_ref, squares_ref):
    own = own_ref[0]
    other = other_ref[0]
    total = dot(own, w_own_ref[...]) + dot(other, w_other_ref[...])
    out_ref[0] = total.astype(BF16)
    squares_ref[0] = lane_sums(own.astype(F32)) + lane_sums(other.astype(F32))


def text_products(order, own, other, w_own, w_other):
    _, rows, feats = own.shape
    count = order.shape[0]
    cols = w_own.shape[1]
    block = pl.BlockSpec((1, rows, feats), lambda i, order: (order[i], 0, 0))
    whole = pl.BlockSpec(w_own.shape, lambda i, order: (0, 0))
    return pl.pallas_call(
        text_kernel,
        out_shape=(
            pltpu.HBM((count, rows, cols), BF16),
            jax.ShapeDtypeStruct((count, 8, rows), F32),
        ),
        grid_spec=pltpu.PrefetchScalarGridSpec(
            num_scalar_prefetch=1,
            grid=(count,),
            in_specs=[block, block, whole, whole],
            out_specs=(
                pl.BlockSpec((1, rows, cols), lambda i, order: (i, 0, 0)),
                pl.BlockSpec((1, 8, rows), lambda i, order: (i, 0, 0)),
            ),
        ),
        compiler_params=PARAMS,
        cost_estimate=pl.CostEstimate(flops=1, bytes_accessed=1, transcendentals=0),
        name="text",
    )(order, in_hbm(own), other, w_own, w_other)


def merged(block, slots_ref, visual, visual_squares, text, text_squares):
    rows = text.shape[0]
    position = lax.broadcasted_iota(jnp.int32, (rows, slots_ref.shape[1]), 0) + block * rows
    hit = (position == slots_ref[0:1, :]).astype(F32)
    is_visual = jnp.sum(hit, axis=1, keepdims=True) > 0.5
    hit = hit.astype(BF16)
    out = jnp.where(is_visual, dot(hit, visual), text.astype(F32))
    parts = jnp.concatenate(
        three_parts(visual_squares) + [jnp.ones((1, hit.shape[1]), F32)]
        + [jnp.zeros((4, hit.shape[1]), F32)],
        axis=0,
    )
    found = lax.dot_general(
        parts.astype(BF16), hit, (((1,), (1,)), ((), ())), preferred_element_type=F32
    )
    squares = jnp.where(found[3:4, :] > 0.5, stripe_sum(found), text_squares)
    return out.astype(BF16), squares


def visual_kernel(
    order_ref, v_own_ref, v_other_ref, w_own_ref, w_other_ref, slots_ref, text_ref, squares_ref,
    visual_ref, vis_squares_ref, key_ref, value_ref,
):
    own = v_own_ref[...]
    other = v_other_ref[...]
    visual = (dot(own, w_own_ref[...]) + dot(other, w_other_ref[...])).astype(BF16)
    visual_ref[...] = visual
    vis_squares = lane_sums(own.astype(F32)) + lane_sums(other.astype(F32))
    vis_squares_ref[...] = vis_squares
    out, squares = merged(
        order_ref[0], slots_ref, visual, vis_squares[0:1, :], text_ref[0], squares_ref[0, 0:1, :]
    )
    rows = out.shape[0]
    cols = key_ref.shape[1]
    key_ref[:rows, :] = out[:, :cols]
    value_ref[...] = out[:, cols:]
    wide = jnp.concatenate([squares, jnp.zeros((1, cols - rows), F32)], axis=1)
    key_ref[rows:, :] = stripe_of(wide)


def visual_products(order, v_own, v_other, w_own, w_other, slots, text, squares):
    _, rows, cols2 = text.shape
    cols = cols2 // 2
    count = v_own.shape[0]
    whole = lambda a: pl.BlockSpec(a.shape, lambda i, order: (0,) * a.ndim)
    shapes = [((count, cols2), BF16), ((8, count), F32), ((rows + STRIPE, cols), BF16), ((rows, cols), BF16)]
    return pl.pallas_call(
        visual_kernel,
        out_shape=tuple(jax.ShapeDtypeStruct(*s) for s in shapes),
        grid_spec=pltpu.PrefetchScalarGridSpec(
            num_scalar_prefetch=1,
            grid=(1,),
            in_specs=[
                whole(v_own),
                whole(v_other),
                whole(w_own),
                whole(w_other),
                whole(slots),
                pl.BlockSpec((1, rows, cols2), lambda i, order: (0, 0, 0)),
                pl.BlockSpec((1, 8, rows), lambda i, order: (0, 0, 0)),
            ],
            out_specs=tuple(pl.BlockSpec(s[0], lambda i, order: (0, 0)) for s in shapes),
        ),
        compiler_params=PARAMS,
        name="visual",
    )(order, v_own, v_other, w_own, w_other, slots, text, squares)


def merge_kernel(
    order_ref, slots_ref, visual_ref, vis_squares_ref, text_ref, squares_ref, out_ref, sums_ref
):
    out, squares = merged(
        order_ref[pl.program_id(0) + 1], slots_ref, visual_ref[...], vis_squares_ref[0:1, :],
        text_ref[0], squares_ref[0, 0:1, :],
    )
    out_ref[0] = out
    sums_ref[0] = jnp.broadcast_to(squares, sums_ref.shape[1:])


def merge(order, slots, visual, vis_squares, text, squares):
    count = text.shape[0] - 1
    _, rows, cols = text.shape
    whole = lambda a: pl.BlockSpec(a.shape, lambda i, order: (0,) * a.ndim)
    later = lambda a: pl.BlockSpec((1,) + a.shape[1:], lambda i, order: (i + 1, 0, 0))
    same = lambda a: pl.BlockSpec((1,) + a.shape[1:], lambda i, order: (i, 0, 0))
    return pl.pallas_call(
        merge_kernel,
        out_shape=(
            jax.ShapeDtypeStruct((count, rows, cols), BF16),
            jax.ShapeDtypeStruct((count, 8, rows), F32),
        ),
        grid_spec=pltpu.PrefetchScalarGridSpec(
            num_scalar_prefetch=1,
            grid=(count,),
            in_specs=[whole(slots), whole(visual), whole(vis_squares), later(text), later(squares)],
            out_specs=(same(text), same(squares)),
        ),
        compiler_params=PARAMS,
        cost_estimate=pl.CostEstimate(
            flops=count * 2 * rows * slots.shape[1] * cols,
            bytes_accessed=count * rows * cols * 4,
            transcendentals=0,
        ),
        name="merge",
    )(order, slots, visual, vis_squares, text, squares)


def stripe_of(squares):
    parts = three_parts(squares)
    pad = jnp.zeros((STRIPE - 3, squares.shape[1]), F32)
    stripe = jnp.concatenate(parts + [pad], axis=0)
    return stripe.astype(BF16)


def stripe_sum(stripe):
    return stripe[0:1] + stripe[1:2] + stripe[2:3]


def hop_kernel(part, came_rows, last, product_ref, squares_ref, came_ref, *out_refs):
    rows = product_ref.shape[1]
    cols = product_ref.shape[2]
    squares = []
    for i in range(2):
        ref = out_refs[i] if last else out_refs[0]
        to = slice(0, rows) if last else slice(i * rows, (i + 1) * rows)
        if i * rows < came_rows:
            came = came_ref[i * rows : (i + 1) * rows, :].astype(F32)
            ref[to, :] = (product_ref[i].astype(F32) + came).astype(BF16)
        else:
            ref[to, :] = product_ref[i]
        squares.append(squares_ref[i, 0:1, :])
    if part == 0:
        sums = jnp.concatenate(squares, axis=1) + stripe_sum(came_ref[came_rows:, :].astype(F32))
        if last:
            pad = jnp.zeros((1, cols - rows), F32)
            for i in range(2):
                wide = jnp.concatenate([sums[:, i * rows : (i + 1) * rows], pad], axis=1)
                out_refs[i][rows:, :] = stripe_of(wide)
        else:
            out_refs[0][2 * rows :, :] = stripe_of(sums)


def hop(part, at, last, product, squares, came):
    rows = product.shape[1]
    cols = product.shape[2] // 2
    extra = STRIPE if part == 0 else 0
    came_rows = came.shape[0] - extra
    shapes = [(rows + extra, cols)] * 2 if last else [(2 * rows + extra, cols)]
    return pl.pallas_call(
        functools.partial(hop_kernel, part, came_rows, last),
        out_shape=tuple(jax.ShapeDtypeStruct(s, BF16) for s in shapes),
        grid=(1,),
        in_specs=[
            pl.BlockSpec(
                (pl.Element(2), pl.Element(rows), pl.Element(cols)), lambda i: (at, 0, part * cols)
            ),
            pl.BlockSpec((pl.Element(2), pl.Element(8), pl.Element(rows)), lambda i: (at, 0, 0)),
            pl.BlockSpec(came.shape, lambda i: (0, 0)),
        ],
        out_specs=tuple(pl.BlockSpec(s, lambda i: (0, 0)) for s in shapes),
        compiler_params=PARAMS,
        name="hop",
    )(product, squares, came)


def finish_kernel(product_ref, squares_ref, k_ref, v_ref, k2_ref, v2_ref, key_ref, value_ref):
    rows = product_ref.shape[1]
    cols = key_ref.shape[1]
    squares = squares_ref[0, 0:1, :]
    squares += stripe_sum(k_ref[rows:, :].astype(F32))[:, :rows]
    squares += stripe_sum(k2_ref[rows:, :].astype(F32))[:, :rows]
    inverse = lax.rsqrt(squares / D + EPS)
    for i in range(rows // LANES):
        to = slice(i * LANES, (i + 1) * LANES)
        scale = jnp.broadcast_to(inverse[:, to], (LANES, LANES)).T
        for out_ref, a_ref, b_ref, at in (
            (key_ref, k_ref, k2_ref, 0),
            (value_ref, v_ref, v2_ref, cols),
        ):
            for j in range(cols // LANES):
                lane = slice(j * LANES, (j + 1) * LANES)
                own = product_ref[0, to, at + j * LANES : at + (j + 1) * LANES].astype(F32)
                total = own + a_ref[to, lane].astype(F32) + b_ref[to, lane].astype(F32)
                out_ref[to, lane] = (total * scale).astype(BF16)


def finish(product, squares, k, v, k2, v2, cols):
    rows = product.shape[1]
    whole = lambda a: pl.BlockSpec(a.shape, lambda i: (0,) * a.ndim)
    last = product.shape[0] - 1
    return pl.pallas_call(
        finish_kernel,
        out_shape=(jax.ShapeDtypeStruct((rows, cols), BF16),) * 2,
        grid=(1,),
        in_specs=[
            pl.BlockSpec((1,) + product.shape[1:], lambda i: (last, 0, 0)),
            pl.BlockSpec((1,) + squares.shape[1:], lambda i: (last, 0, 0)),
        ]
        + [whole(a) for a in (k, v, k2, v2)],
        out_specs=(pl.BlockSpec((rows, cols), lambda i: (0, 0)),) * 2,
        compiler_params=PARAMS,
        name="finish",
    )(product, squares, k, v, k2, v2)


def local(vis_feats, proj_w, text_embed, dest_group, layout, norm_gain, key_w, value_w):
    n_grp = lax.axis_size("grp")
    n_y = lax.axis_size("y")
    h = lax.axis_index("grp")
    y = lax.axis_index("y")
    c = lax.axis_index("core")
    seq_len, feats = text_embed.shape
    rows = seq_len // (2 * n_y)
    tokens = vis_feats.shape[0]
    run_count = n_grp // 2
    capacity = tokens // run_count
    slot_count = n_grp * capacity
    cols = key_w.shape[1]
    swap = [(0, 1), (1, 0)]
    ring = []
    cross = []
    for i in range(n_y):
        above = 2 * ((i + 1) % n_y)
        below = 2 * ((i - 1) % n_y)
        ring += [(2 * i, above), (2 * i + 1, below + 1)]
        cross += [(2 * i, above + 1), (2 * i + 1, below)]

    group = jnp.full((1,), h, jnp.int32)
    dest = dest_group.reshape(-1, LANES)
    outgoing = source(group, dest, vis_feats, proj_w, slot_count, capacity)
    arrived = lax.all_to_all(
        outgoing.reshape(n_grp, capacity, feats), "grp", 0, 0, tiled=True
    ).reshape(slot_count, feats)

    weight = jnp.concatenate([key_w, value_w], axis=1).astype(F32) * norm_gain[:, None]
    weight = weight.astype(BF16)
    blocks = text_embed.reshape(2 * n_y, rows, feats)
    other = lax.ppermute(blocks, "core", swap)
    w_other = lax.ppermute(weight, "core", swap)

    far = n_y // 2
    offset = [far] + [o for o in range(far - 1, 0, -1) for _ in (0, 1)] + [0]
    second = [0] + [0, 1] * (far - 1) + [0]
    offset = jnp.asarray(offset, jnp.int32)
    second = jnp.asarray(second, jnp.int32)
    up = 2 * ((y + offset) % n_y) + second
    down = 2 * ((y - offset + n_y) % n_y) + 1 - second
    mine = jnp.where(c == 0, up, down)
    slots = slot_positions(group, dest, layout, slot_count, capacity, tokens // LANES)
    text, text_squares = text_products(mine, blocks, other, weight, w_other)
    text = in_hbm(text)

    arrived, text_squares, slots = lax.optimization_barrier((arrived, text_squares, slots))
    arrived_other = lax.ppermute(arrived, "core", swap)
    visual, visual_squares, key_leaf, value_leaf = visual_products(
        mine, arrived, arrived_other, weight, w_other, slots, text, text_squares
    )
    flat = ("y", "core")
    streams = [lax.ppermute(key_leaf, flat, ring), lax.ppermute(value_leaf, flat, ring)]
    product, squares = merge(mine, slots, visual, visual_squares, text, text_squares)
    ends = []
    for step in range(far - 1):
        last = step == far - 2
        for part in range(2):
            sent = hop(part, 2 * step, last, product, squares, streams[part])
            streams[part] = lax.ppermute(sent[0], flat, ring)
            if last:
                ends.append(lax.ppermute(sent[1], flat, cross))
    return finish(product, squares, streams[0], streams[1], ends[0], ends[1], cols)


def solution(mesh):
    n_grp, n_sp = mesh.devices.shape
    split = Mesh(mesh.devices.reshape(n_grp, n_sp // 2, 2), ("grp", "y", "core"))
    sp = ("y", "core")
    return jax.shard_map(
        local,
        mesh=split,
        in_specs=(
            P("grp", None),
            P(None, sp),
            P("grp", sp),
            P(),
            P("grp", None),
            P(sp),
            P(sp, None),
            P(sp, None),
        ),
        out_specs=(P(("grp", "y", "core"), None), P(("grp", "y", "core"), None)),
        check_vma=False,
    )
```

```python
import functools

import jax
import jax.numpy as jnp
from jax import lax
from jax.experimental import pallas as pl
from jax.experimental.pallas import tpu as pltpu
from jax.sharding import Mesh
from jax.sharding import PartitionSpec as P

D = 4096
LANES = 128
STRIPE = 16
EPS = 1e-05
F32 = jnp.float32
BF16 = jnp.bfloat16
PARAMS = pltpu.CompilerParams(vmem_limit_bytes=32 * 2**20)


def vmem(n):
    return [pl.BlockSpec(memory_space=pltpu.VMEM)] * n


def in_hbm(x):
    return pltpu.with_memory_space_constraint(x, pltpu.HBM)


def hbm_out(shape, dtype):
    return pltpu.HBM(shape, dtype)


def one_hot(mask):
    return mask.astype(F32).astype(BF16)


def dot(a, b):
    return jnp.dot(a, b, preferred_element_type=F32)


def three_parts(x):
    hi = x.astype(BF16).astype(F32)
    rest = x - hi
    mid = rest.astype(BF16).astype(F32)
    low = (rest - mid).astype(BF16).astype(F32)
    return [hi, mid, low]


def source_kernel(capacity, group_ref, dest_ref, feats_ref, proj_ref, out_ref):
    lines = feats_ref.shape[0] // LANES
    projected = dot(feats_ref[...], proj_ref[...]).astype(BF16)
    first = lax.rem(group_ref[0] * lines, dest_ref.shape[0])
    lane = lax.broadcasted_iota(jnp.int32, (1, LANES), 1)
    slot = lax.broadcasted_iota(jnp.int32, (out_ref.shape[0], LANES), 0)
    places = []
    for i in range(lines):
        target = dest_ref[pl.ds(first + i, 1), :] * capacity + lax.rem(lane, capacity)
        places.append(one_hot(slot == target))
    out_ref[...] = dot(jnp.concatenate(places, axis=1), projected).astype(BF16)


def source(group, dest, feats, proj, slots, capacity):
    tokens = feats.shape[0]
    cols = proj.shape[1]
    lines = tokens // LANES
    return pl.pallas_call(
        functools.partial(source_kernel, capacity),
        out_shape=hbm_out((slots, cols), BF16),
        grid_spec=pltpu.PrefetchScalarGridSpec(
            num_scalar_prefetch=1,
            grid=(1,),
            in_specs=[
                pl.BlockSpec((8, LANES), lambda i, group: (group[0] * lines // 8, 0)),
                pl.BlockSpec(feats.shape, lambda i, group: (0, 0)),
                pl.BlockSpec(proj.shape, lambda i, group: (0, 0)),
            ],
            out_specs=pl.BlockSpec((slots, cols), lambda i, group: (0, 0)),
        ),
        compiler_params=PARAMS,
        name="source",
    )(group, in_hbm(dest), in_hbm(feats), in_hbm(proj))


def slots_kernel(capacity, lines, group_ref, dest_ref, layout_ref, out_ref):
    slots = out_ref.shape[1]
    hits = one_hot(dest_ref[...] == group_ref[0])
    ones = jnp.ones((8, LANES), BF16)
    counts = lax.dot_general(
        ones, hits, (((1,), (1,)), ((), ())), preferred_element_type=F32
    ).astype(BF16)
    shape = (dest_ref.shape[0], slots)
    sender = lax.div(lax.broadcasted_iota(jnp.int32, shape, 0), lines)
    slot = lax.div(lax.broadcasted_iota(jnp.int32, shape, 1), capacity)
    before = dot(counts, one_hot(sender < slot)).astype(jnp.int32)
    sends = dot(counts, one_hot(sender == slot))
    token = lax.rem(lax.broadcasted_iota(jnp.int32, (1, slots), 1), capacity)
    rank = lax.broadcasted_iota(jnp.int32, (slots, slots), 0)
    chosen = one_hot(rank == before[0:1, :] + token)
    order = layout_ref[...]
    high = lax.div(order, 64)
    both = jnp.concatenate(
        [high.astype(F32), (order - high * 64).astype(F32), jnp.zeros((6, slots), F32)], axis=0
    )
    found = dot(both.astype(BF16), chosen).astype(jnp.int32)
    place = found[0:1, :] * 64 + found[1:2, :]
    place = jnp.where(sends[0:1, :] > 0.5, place, -1)
    out_ref[...] = jnp.broadcast_to(place, out_ref.shape)


def slot_positions(group, dest, layout, slots, capacity, lines):
    return pl.pallas_call(
        functools.partial(slots_kernel, capacity, lines),
        out_shape=jax.ShapeDtypeStruct((8, slots), jnp.int32),
        grid_spec=pltpu.PrefetchScalarGridSpec(
            num_scalar_prefetch=1,
            grid=(1,),
            in_specs=[
                pl.BlockSpec(dest.shape, lambda i, group: (0, 0)),
                pl.BlockSpec((1, slots), lambda i, group: (0, 0)),
            ],
            out_specs=pl.BlockSpec((8, slots), lambda i, group: (0, 0)),
        ),
        compiler_params=PARAMS,
        cost_estimate=pl.CostEstimate(flops=1, bytes_accessed=1, transcendentals=0),
        name="slots",
    )(group, dest, layout)


def lane_sums(x):
    square = x * x
    hi = square.astype(BF16)
    low = (square - hi.astype(F32)).astype(BF16)
    ones = jnp.ones((8, x.shape[1]), BF16)
    dims = (((1,), (1,)), ((), ()))
    total = lax.dot_general(ones, hi, dims, preferred_element_type=F32)
    return total + lax.dot_general(ones, low, dims, preferred_element_type=F32)


def text_kernel(order_ref, own_ref, other_ref, w_own_ref, w_other_ref, out_ref, squares_ref):
    own = own_ref[0]
    other = other_ref[0]
    total = dot(own, w_own_ref[...]) + dot(other, w_other_ref[...])
    out_ref[0] = total.astype(BF16)
    squares_ref[0] = lane_sums(own.astype(F32)) + lane_sums(other.astype(F32))


def text_products(order, own, other, w_own, w_other):
    _, rows, feats = own.shape
    count = order.shape[0]
    cols = w_own.shape[1]
    block = pl.BlockSpec((1, rows, feats), lambda i, order: (order[i], 0, 0))
    whole = pl.BlockSpec(w_own.shape, lambda i, order: (0, 0))
    return pl.pallas_call(
        text_kernel,
        out_shape=(
            hbm_out((count, rows, cols), BF16),
            jax.ShapeDtypeStruct((count, 8, rows), F32),
        ),
        grid_spec=pltpu.PrefetchScalarGridSpec(
            num_scalar_prefetch=1,
            grid=(count,),
            in_specs=[block, block, whole, whole],
            out_specs=(
                pl.BlockSpec((1, rows, cols), lambda i, order: (i, 0, 0)),
                pl.BlockSpec((1, 8, rows), lambda i, order: (i, 0, 0)),
            ),
        ),
        compiler_params=PARAMS,
        cost_estimate=pl.CostEstimate(flops=1, bytes_accessed=1, transcendentals=0),
        name="text",
    )(order, in_hbm(own), other, w_own, w_other)


def merged(block, slots_ref, visual, visual_squares, text, text_squares):
    rows = text.shape[0]
    position = lax.broadcasted_iota(jnp.int32, (rows, slots_ref.shape[1]), 0) + block * rows
    hit = (position == slots_ref[0:1, :]).astype(F32)
    is_visual = jnp.sum(hit, axis=1, keepdims=True) > 0.5
    hit = hit.astype(BF16)
    out = jnp.where(is_visual, dot(hit, visual), text.astype(F32))
    parts = jnp.concatenate(
        three_parts(visual_squares) + [jnp.ones((1, hit.shape[1]), F32)]
        + [jnp.zeros((4, hit.shape[1]), F32)],
        axis=0,
    )
    found = lax.dot_general(
        parts.astype(BF16), hit, (((1,), (1,)), ((), ())), preferred_element_type=F32
    )
    squares = jnp.where(found[3:4, :] > 0.5, stripe_sum(found), text_squares)
    return out.astype(BF16), squares


def visual_kernel(
    order_ref, v_own_ref, v_other_ref, w_own_ref, w_other_ref, slots_ref, text_ref, squares_ref,
    visual_ref, vis_squares_ref, key_ref, value_ref,
):
    own = v_own_ref[...]
    other = v_other_ref[...]
    visual = (dot(own, w_own_ref[...]) + dot(other, w_other_ref[...])).astype(BF16)
    visual_ref[...] = visual
    vis_squares = lane_sums(own.astype(F32)) + lane_sums(other.astype(F32))
    vis_squares_ref[...] = vis_squares
    out, squares = merged(
        order_ref[0], slots_ref, visual, vis_squares[0:1, :], text_ref[0], squares_ref[0, 0:1, :]
    )
    rows = out.shape[0]
    cols = key_ref.shape[1]
    key_ref[:rows, :] = out[:, :cols]
    value_ref[...] = out[:, cols:]
    wide = jnp.concatenate([squares, jnp.zeros((1, cols - rows), F32)], axis=1)
    key_ref[rows:, :] = stripe_of(wide)


def visual_products(order, v_own, v_other, w_own, w_other, slots, text, squares):
    _, rows, cols2 = text.shape
    cols = cols2 // 2
    count = v_own.shape[0]
    whole = lambda a: pl.BlockSpec(a.shape, lambda i, order: (0,) * a.ndim)
    shapes = [((count, cols2), BF16), ((8, count), F32), ((rows + STRIPE, cols), BF16), ((rows, cols), BF16)]
    return pl.pallas_call(
        visual_kernel,
        out_shape=tuple(jax.ShapeDtypeStruct(*s) for s in shapes),
        grid_spec=pltpu.PrefetchScalarGridSpec(
            num_scalar_prefetch=1,
            grid=(1,),
            in_specs=[
                whole(v_own),
                whole(v_other),
                whole(w_own),
                whole(w_other),
                whole(slots),
                pl.BlockSpec((1, rows, cols2), lambda i, order: (0, 0, 0)),
                pl.BlockSpec((1, 8, rows), lambda i, order: (0, 0, 0)),
            ],
            out_specs=tuple(pl.BlockSpec(s[0], lambda i, order: (0, 0)) for s in shapes),
        ),
        compiler_params=PARAMS,
        name="visual",
    )(order, v_own, v_other, w_own, w_other, slots, text, squares)


def merge_kernel(
    first, order_ref, slots_ref, visual_ref, vis_squares_ref, text_ref, squares_ref, out_ref, sums_ref
):
    out, squares = merged(
        order_ref[pl.program_id(0) + first], slots_ref, visual_ref[...], vis_squares_ref[0:1, :],
        text_ref[0], squares_ref[0, 0:1, :],
    )
    out_ref[0] = out
    sums_ref[0] = jnp.broadcast_to(squares, sums_ref.shape[1:])


def merge(first, count, order, slots, visual, vis_squares, text, squares):
    _, rows, cols = text.shape
    whole = lambda a: pl.BlockSpec(a.shape, lambda i, order: (0,) * a.ndim)
    later = lambda a: pl.BlockSpec((1,) + a.shape[1:], lambda i, order: (i + first, 0, 0))
    same = lambda a: pl.BlockSpec((1,) + a.shape[1:], lambda i, order: (i, 0, 0))
    return pl.pallas_call(
        functools.partial(merge_kernel, first),
        out_shape=(
            jax.ShapeDtypeStruct((count, rows, cols), BF16),
            jax.ShapeDtypeStruct((count, 8, rows), F32),
        ),
        grid_spec=pltpu.PrefetchScalarGridSpec(
            num_scalar_prefetch=1,
            grid=(count,),
            in_specs=[whole(slots), whole(visual), whole(vis_squares), later(text), later(squares)],
            out_specs=(same(text), same(squares)),
        ),
        compiler_params=PARAMS,
        cost_estimate=pl.CostEstimate(
            flops=count * 2 * rows * slots.shape[1] * cols,
            bytes_accessed=count * rows * cols * 4,
            transcendentals=0,
        ),
        name="merge",
    )(order, slots, visual, vis_squares, text, squares)


def stripe_of(squares):
    parts = three_parts(squares)
    pad = jnp.zeros((STRIPE - 3, squares.shape[1]), F32)
    stripe = jnp.concatenate(parts + [pad], axis=0)
    return stripe.astype(BF16)


def stripe_sum(stripe):
    return stripe[0:1] + stripe[1:2] + stripe[2:3]


def hop_kernel(part, came_rows, last, product_ref, squares_ref, came_ref, *out_refs):
    rows = product_ref.shape[1]
    cols = product_ref.shape[2]
    squares = []
    for i in range(2):
        ref = out_refs[i] if last else out_refs[0]
        to = slice(0, rows) if last else slice(i * rows, (i + 1) * rows)
        if i * rows < came_rows:
            came = came_ref[i * rows : (i + 1) * rows, :].astype(F32)
            ref[to, :] = (product_ref[i].astype(F32) + came).astype(BF16)
        else:
            ref[to, :] = product_ref[i]
        squares.append(squares_ref[i, 0:1, :])
    if part == 0:
        sums = jnp.concatenate(squares, axis=1) + stripe_sum(came_ref[came_rows:, :].astype(F32))
        if last:
            pad = jnp.zeros((1, cols - rows), F32)
            for i in range(2):
                wide = jnp.concatenate([sums[:, i * rows : (i + 1) * rows], pad], axis=1)
                out_refs[i][rows:, :] = stripe_of(wide)
        else:
            out_refs[0][2 * rows :, :] = stripe_of(sums)


def hop(part, at, last, product, squares, came):
    rows = product.shape[1]
    cols = product.shape[2] // 2
    extra = STRIPE if part == 0 else 0
    came_rows = came.shape[0] - extra
    shapes = [(rows + extra, cols)] * 2 if last else [(2 * rows + extra, cols)]
    return pl.pallas_call(
        functools.partial(hop_kernel, part, came_rows, last),
        out_shape=tuple(jax.ShapeDtypeStruct(s, BF16) for s in shapes),
        grid=(1,),
        in_specs=[
            pl.BlockSpec(
                (pl.Element(2), pl.Element(rows), pl.Element(cols)), lambda i: (at, 0, part * cols)
            ),
            pl.BlockSpec((pl.Element(2), pl.Element(8), pl.Element(rows)), lambda i: (at, 0, 0)),
            pl.BlockSpec(came.shape, lambda i: (0, 0)),
        ],
        out_specs=tuple(pl.BlockSpec(s, lambda i: (0, 0)) for s in shapes),
        compiler_params=PARAMS,
        name="hop",
    )(product, squares, came)


def finish_kernel(product_ref, squares_ref, k_ref, v_ref, k2_ref, v2_ref, key_ref, value_ref):
    rows = product_ref.shape[1]
    cols = key_ref.shape[1]
    squares = squares_ref[0, 0:1, :]
    squares += stripe_sum(k_ref[rows:, :].astype(F32))[:, :rows]
    squares += stripe_sum(k2_ref[rows:, :].astype(F32))[:, :rows]
    inverse = lax.rsqrt(squares / D + EPS)
    for i in range(rows // LANES):
        to = slice(i * LANES, (i + 1) * LANES)
        scale = jnp.broadcast_to(inverse[:, to], (LANES, LANES)).T
        for out_ref, a_ref, b_ref, at in (
            (key_ref, k_ref, k2_ref, 0),
            (value_ref, v_ref, v2_ref, cols),
        ):
            for j in range(cols // LANES):
                lane = slice(j * LANES, (j + 1) * LANES)
                own = product_ref[0, to, at + j * LANES : at + (j + 1) * LANES].astype(F32)
                total = own + a_ref[to, lane].astype(F32) + b_ref[to, lane].astype(F32)
                out_ref[to, lane] = (total * scale).astype(BF16)


def finish(product, squares, k, v, k2, v2, cols):
    rows = product.shape[1]
    whole = lambda a: pl.BlockSpec(a.shape, lambda i: (0,) * a.ndim)
    last = product.shape[0] - 1
    return pl.pallas_call(
        finish_kernel,
        out_shape=(jax.ShapeDtypeStruct((rows, cols), BF16),) * 2,
        grid=(1,),
        in_specs=[
            pl.BlockSpec((1,) + product.shape[1:], lambda i: (last, 0, 0)),
            pl.BlockSpec((1,) + squares.shape[1:], lambda i: (last, 0, 0)),
        ]
        + [whole(a) for a in (k, v, k2, v2)],
        out_specs=(pl.BlockSpec((rows, cols), lambda i: (0, 0)),) * 2,
        compiler_params=PARAMS,
        name="finish",
    )(product, squares, k, v, k2, v2)


def local(vis_feats, proj_w, text_embed, dest_group, layout, norm_gain, key_w, value_w):
    n_grp = lax.axis_size("grp")
    n_y = lax.axis_size("y")
    h = lax.axis_index("grp")
    y = lax.axis_index("y")
    c = lax.axis_index("core")
    seq_len, feats = text_embed.shape
    rows = seq_len // (2 * n_y)
    tokens = vis_feats.shape[0]
    run_count = n_grp // 2
    capacity = tokens // run_count
    slot_count = n_grp * capacity
    cols = key_w.shape[1]
    swap = [(0, 1), (1, 0)]
    ring = []
    cross = []
    for i in range(n_y):
        above = 2 * ((i + 1) % n_y)
        below = 2 * ((i - 1) % n_y)
        ring += [(2 * i, above), (2 * i + 1, below + 1)]
        cross += [(2 * i, above + 1), (2 * i + 1, below)]

    group = jnp.full((1,), h, jnp.int32)
    dest = dest_group.reshape(-1, LANES)
    outgoing = source(group, dest, vis_feats, proj_w, slot_count, capacity)
    arrived = lax.all_to_all(
        outgoing.reshape(n_grp, capacity, feats), "grp", 0, 0, tiled=True
    ).reshape(slot_count, feats)

    weight = jnp.concatenate([key_w, value_w], axis=1).astype(F32) * norm_gain[:, None]
    weight = weight.astype(BF16)
    w_other = lax.ppermute(weight, "core", swap)
    blocks = text_embed.reshape(2 * n_y, rows, feats)
    other = lax.ppermute(blocks, "core", swap)

    far = n_y // 2
    offset = [far] + [o for o in range(far - 1, 0, -1) for _ in (0, 1)] + [0]
    second = [0] + [0, 1] * (far - 1) + [0]
    offset = jnp.asarray(offset, jnp.int32)
    second = jnp.asarray(second, jnp.int32)
    up = 2 * ((y + offset) % n_y) + second
    down = 2 * ((y - offset + n_y) % n_y) + 1 - second
    mine = jnp.where(c == 0, up, down)
    slots = slot_positions(group, dest, layout, slot_count, capacity, tokens // LANES)
    text, text_squares = text_products(mine, blocks, other, weight, w_other)
    text = in_hbm(text)

    arrived, text_squares, slots = lax.optimization_barrier((arrived, text_squares, slots))
    arrived_other = lax.ppermute(arrived, "core", swap)
    visual, visual_squares, key_leaf, value_leaf = visual_products(
        mine, arrived, arrived_other, weight, w_other, slots, text, text_squares
    )
    flat = ("y", "core")
    streams = [lax.ppermute(key_leaf, flat, ring), lax.ppermute(value_leaf, flat, ring)]
    merged_blocks = merge(1, 2, mine, slots, visual, visual_squares, text, text_squares)
    ends = []
    for step in range(far - 1):
        last = step == far - 2
        at = 0 if step == 0 else 2 * step - 2
        sends = [hop(part, at, last, *merged_blocks, streams[part]) for part in range(2)]
        for part in range(2):
            streams[part] = lax.ppermute(sends[part][0], flat, ring)
            if last:
                ends.append(lax.ppermute(sends[part][1], flat, cross))
        if step == 0:
            slots, _, _ = lax.optimization_barrier((slots, sends[0][0], sends[1][0]))
            merged_blocks = merge(
                3, n_y - 3, mine, slots, visual, visual_squares, text, text_squares
            )
    return finish(*merged_blocks, streams[0], streams[1], ends[0], ends[1], cols)


def solution(mesh):
    n_grp, n_sp = mesh.devices.shape
    split = Mesh(mesh.devices.reshape(n_grp, n_sp // 2, 2), ("grp", "y", "core"))
    sp = ("y", "core")
    return jax.shard_map(
        local,
        mesh=split,
        in_specs=(
            P("grp", None),
            P(None, sp),
            P("grp", sp),
            P(),
            P("grp", None),
            P(sp),
            P(sp, None),
            P(sp, None),
        ),
        out_specs=(P(("grp", "y", "core"), None), P(("grp", "y", "core"), None)),
        check_vma=False,
    )
```

```python
import functools

import jax
import jax.numpy as jnp
from jax import lax
from jax.experimental import pallas as pl
from jax.experimental.pallas import tpu as pltpu
from jax.sharding import Mesh
from jax.sharding import PartitionSpec as P

D = 4096
LANES = 128
STRIPE = 16
EPS = 1e-05
F32 = jnp.float32
BF16 = jnp.bfloat16
PARAMS = pltpu.CompilerParams(vmem_limit_bytes=32 * 2**20)


def vmem(n):
    return [pl.BlockSpec(memory_space=pltpu.VMEM)] * n


def in_hbm(x):
    return pltpu.with_memory_space_constraint(x, pltpu.HBM)


def hbm_out(shape, dtype):
    return pltpu.HBM(shape, dtype)


def one_hot(mask):
    return mask.astype(F32).astype(BF16)


def dot(a, b):
    return jnp.dot(a, b, preferred_element_type=F32)


def three_parts(x):
    hi = x.astype(BF16).astype(F32)
    rest = x - hi
    mid = rest.astype(BF16).astype(F32)
    low = (rest - mid).astype(BF16).astype(F32)
    return [hi, mid, low]


def source_kernel(capacity, group_ref, dest_ref, feats_ref, proj_ref, out_ref):
    lines = feats_ref.shape[0] // LANES
    projected = dot(feats_ref[...], proj_ref[...]).astype(BF16)
    first = lax.rem(group_ref[0] * lines, dest_ref.shape[0])
    lane = lax.broadcasted_iota(jnp.int32, (1, LANES), 1)
    slot = lax.broadcasted_iota(jnp.int32, (out_ref.shape[0], LANES), 0)
    places = []
    for i in range(lines):
        target = dest_ref[pl.ds(first + i, 1), :] * capacity + lax.rem(lane, capacity)
        places.append(one_hot(slot == target))
    out_ref[...] = dot(jnp.concatenate(places, axis=1), projected).astype(BF16)


def source(group, dest, feats, proj, slots, capacity):
    tokens = feats.shape[0]
    cols = proj.shape[1]
    lines = tokens // LANES
    return pl.pallas_call(
        functools.partial(source_kernel, capacity),
        out_shape=hbm_out((slots, cols), BF16),
        grid_spec=pltpu.PrefetchScalarGridSpec(
            num_scalar_prefetch=1,
            grid=(1,),
            in_specs=[
                pl.BlockSpec((8, LANES), lambda i, group: (group[0] * lines // 8, 0)),
                pl.BlockSpec(feats.shape, lambda i, group: (0, 0)),
                pl.BlockSpec(proj.shape, lambda i, group: (0, 0)),
            ],
            out_specs=pl.BlockSpec((slots, cols), lambda i, group: (0, 0)),
        ),
        compiler_params=PARAMS,
        name="source",
    )(group, in_hbm(dest), in_hbm(feats), in_hbm(proj))


def slots_kernel(capacity, lines, group_ref, dest_ref, layout_ref, out_ref):
    slots = out_ref.shape[1]
    hits = one_hot(dest_ref[...] == group_ref[0])
    ones = jnp.ones((8, LANES), BF16)
    counts = lax.dot_general(
        ones, hits, (((1,), (1,)), ((), ())), preferred_element_type=F32
    ).astype(BF16)
    shape = (dest_ref.shape[0], slots)
    sender = lax.div(lax.broadcasted_iota(jnp.int32, shape, 0), lines)
    slot = lax.div(lax.broadcasted_iota(jnp.int32, shape, 1), capacity)
    before = dot(counts, one_hot(sender < slot)).astype(jnp.int32)
    sends = dot(counts, one_hot(sender == slot))
    token = lax.rem(lax.broadcasted_iota(jnp.int32, (1, slots), 1), capacity)
    rank = lax.broadcasted_iota(jnp.int32, (slots, slots), 0)
    chosen = one_hot(rank == before[0:1, :] + token)
    order = layout_ref[...]
    high = lax.div(order, 64)
    both = jnp.concatenate(
        [high.astype(F32), (order - high * 64).astype(F32), jnp.zeros((6, slots), F32)], axis=0
    )
    found = dot(both.astype(BF16), chosen).astype(jnp.int32)
    place = found[0:1, :] * 64 + found[1:2, :]
    place = jnp.where(sends[0:1, :] > 0.5, place, -1)
    out_ref[...] = jnp.broadcast_to(place, out_ref.shape)


def slot_positions(group, dest, layout, slots, capacity, lines):
    return pl.pallas_call(
        functools.partial(slots_kernel, capacity, lines),
        out_shape=jax.ShapeDtypeStruct((8, slots), jnp.int32),
        grid_spec=pltpu.PrefetchScalarGridSpec(
            num_scalar_prefetch=1,
            grid=(1,),
            in_specs=[
                pl.BlockSpec(dest.shape, lambda i, group: (0, 0)),
                pl.BlockSpec((1, slots), lambda i, group: (0, 0)),
            ],
            out_specs=pl.BlockSpec((8, slots), lambda i, group: (0, 0)),
        ),
        compiler_params=PARAMS,
        cost_estimate=pl.CostEstimate(flops=1, bytes_accessed=1, transcendentals=0),
        name="slots",
    )(group, dest, layout)


def lane_sums(x):
    square = x * x
    hi = square.astype(BF16)
    low = (square - hi.astype(F32)).astype(BF16)
    ones = jnp.ones((8, x.shape[1]), BF16)
    dims = (((1,), (1,)), ((), ()))
    total = lax.dot_general(ones, hi, dims, preferred_element_type=F32)
    return total + lax.dot_general(ones, low, dims, preferred_element_type=F32)


def text_kernel(order_ref, own_ref, other_ref, w_own_ref, w_other_ref, out_ref, squares_ref):
    own = own_ref[0]
    other = other_ref[0]
    total = dot(own, w_own_ref[...]) + dot(other, w_other_ref[...])
    out_ref[0] = total.astype(BF16)
    squares_ref[0] = lane_sums(own.astype(F32)) + lane_sums(other.astype(F32))


def text_products(order, own, other, w_own, w_other):
    _, rows, feats = own.shape
    count = order.shape[0]
    cols = w_own.shape[1]
    block = pl.BlockSpec((1, rows, feats), lambda i, order: (order[i], 0, 0))
    whole = pl.BlockSpec(w_own.shape, lambda i, order: (0, 0))
    return pl.pallas_call(
        text_kernel,
        out_shape=(
            hbm_out((count, rows, cols), BF16),
            jax.ShapeDtypeStruct((count, 8, rows), F32),
        ),
        grid_spec=pltpu.PrefetchScalarGridSpec(
            num_scalar_prefetch=1,
            grid=(count,),
            in_specs=[block, block, whole, whole],
            out_specs=(
                pl.BlockSpec((1, rows, cols), lambda i, order: (i, 0, 0)),
                pl.BlockSpec((1, 8, rows), lambda i, order: (i, 0, 0)),
            ),
        ),
        compiler_params=PARAMS,
        cost_estimate=pl.CostEstimate(flops=1, bytes_accessed=1, transcendentals=0),
        name="text",
    )(order, in_hbm(own), other, w_own, w_other)


def merged(block, slots_ref, visual, visual_squares, text, text_squares):
    rows = text.shape[0]
    position = lax.broadcasted_iota(jnp.int32, (rows, slots_ref.shape[1]), 0) + block * rows
    hit = (position == slots_ref[0:1, :]).astype(F32)
    is_visual = jnp.sum(hit, axis=1, keepdims=True) > 0.5
    hit = hit.astype(BF16)
    out = jnp.where(is_visual, dot(hit, visual), text.astype(F32))
    parts = jnp.concatenate(
        three_parts(visual_squares) + [jnp.ones((1, hit.shape[1]), F32)]
        + [jnp.zeros((4, hit.shape[1]), F32)],
        axis=0,
    )
    found = lax.dot_general(
        parts.astype(BF16), hit, (((1,), (1,)), ((), ())), preferred_element_type=F32
    )
    squares = jnp.where(found[3:4, :] > 0.5, stripe_sum(found), text_squares)
    return out.astype(BF16), squares


def own_kernel(tokens_ref, weight_ref, out_ref, squares_ref):
    tokens = tokens_ref[...]
    out_ref[...] = dot(tokens, weight_ref[...])
    squares_ref[...] = lane_sums(tokens.astype(F32))


def own_products(tokens, weight):
    return pl.pallas_call(
        own_kernel,
        out_shape=(
            jax.ShapeDtypeStruct((tokens.shape[0], weight.shape[1]), F32),
            jax.ShapeDtypeStruct((8, tokens.shape[0]), F32),
        ),
        in_specs=vmem(2),
        out_specs=tuple(vmem(2)),
        compiler_params=PARAMS,
        name="own",
    )(tokens, weight)


def visual_kernel(
    order_ref, own_ref, own_squares_ref, v_other_ref, w_other_ref, slots_ref, text_ref, squares_ref,
    visual_ref, vis_squares_ref, key_ref, value_ref,
):
    other = v_other_ref[...]
    visual = (own_ref[...] + dot(other, w_other_ref[...])).astype(BF16)
    visual_ref[...] = visual
    vis_squares = own_squares_ref[...] + lane_sums(other.astype(F32))
    vis_squares_ref[...] = vis_squares
    out, squares = merged(
        order_ref[0], slots_ref, visual, vis_squares[0:1, :], text_ref[0], squares_ref[0, 0:1, :]
    )
    rows = out.shape[0]
    cols = key_ref.shape[1]
    key_ref[:rows, :] = out[:, :cols]
    value_ref[...] = out[:, cols:]
    wide = jnp.concatenate([squares, jnp.zeros((1, cols - rows), F32)], axis=1)
    key_ref[rows:, :] = stripe_of(wide)


def visual_products(order, own, own_squares, v_other, w_other, slots, text, squares):
    _, rows, cols2 = text.shape
    cols = cols2 // 2
    count = v_other.shape[0]
    whole = lambda a: pl.BlockSpec(a.shape, lambda i, order: (0,) * a.ndim)
    shapes = [((count, cols2), BF16), ((8, count), F32), ((rows + STRIPE, cols), BF16), ((rows, cols), BF16)]
    return pl.pallas_call(
        visual_kernel,
        out_shape=tuple(jax.ShapeDtypeStruct(*s) for s in shapes),
        grid_spec=pltpu.PrefetchScalarGridSpec(
            num_scalar_prefetch=1,
            grid=(1,),
            in_specs=[
                whole(own),
                whole(own_squares),
                whole(v_other),
                whole(w_other),
                whole(slots),
                pl.BlockSpec((1, rows, cols2), lambda i, order: (0, 0, 0)),
                pl.BlockSpec((1, 8, rows), lambda i, order: (0, 0, 0)),
            ],
            out_specs=tuple(pl.BlockSpec(s[0], lambda i, order: (0, 0)) for s in shapes),
        ),
        compiler_params=PARAMS,
        name="visual",
    )(order, own, own_squares, v_other, w_other, slots, text, squares)


def merge_kernel(
    first, order_ref, slots_ref, visual_ref, vis_squares_ref, text_ref, squares_ref, out_ref, sums_ref
):
    out, squares = merged(
        order_ref[pl.program_id(0) + first], slots_ref, visual_ref[...], vis_squares_ref[0:1, :],
        text_ref[0], squares_ref[0, 0:1, :],
    )
    out_ref[0] = out
    sums_ref[0] = jnp.broadcast_to(squares, sums_ref.shape[1:])


def merge(first, count, order, slots, visual, vis_squares, text, squares):
    _, rows, cols = text.shape
    whole = lambda a: pl.BlockSpec(a.shape, lambda i, order: (0,) * a.ndim)
    later = lambda a: pl.BlockSpec((1,) + a.shape[1:], lambda i, order: (i + first, 0, 0))
    same = lambda a: pl.BlockSpec((1,) + a.shape[1:], lambda i, order: (i, 0, 0))
    return pl.pallas_call(
        functools.partial(merge_kernel, first),
        out_shape=(
            jax.ShapeDtypeStruct((count, rows, cols), BF16),
            jax.ShapeDtypeStruct((count, 8, rows), F32),
        ),
        grid_spec=pltpu.PrefetchScalarGridSpec(
            num_scalar_prefetch=1,
            grid=(count,),
            in_specs=[whole(slots), whole(visual), whole(vis_squares), later(text), later(squares)],
            out_specs=(same(text), same(squares)),
        ),
        compiler_params=PARAMS,
        cost_estimate=pl.CostEstimate(
            flops=count * 2 * rows * slots.shape[1] * cols,
            bytes_accessed=count * rows * cols * 4,
            transcendentals=0,
        ),
        name="merge",
    )(order, slots, visual, vis_squares, text, squares)


def stripe_of(squares):
    parts = three_parts(squares)
    pad = jnp.zeros((STRIPE - 3, squares.shape[1]), F32)
    stripe = jnp.concatenate(parts + [pad], axis=0)
    return stripe.astype(BF16)


def stripe_sum(stripe):
    return stripe[0:1] + stripe[1:2] + stripe[2:3]


def hop_kernel(part, came_rows, last, product_ref, squares_ref, came_ref, *out_refs):
    rows = product_ref.shape[1]
    cols = product_ref.shape[2]
    squares = []
    for i in range(2):
        ref = out_refs[i] if last else out_refs[0]
        to = slice(0, rows) if last else slice(i * rows, (i + 1) * rows)
        if i * rows < came_rows:
            came = came_ref[i * rows : (i + 1) * rows, :].astype(F32)
            ref[to, :] = (product_ref[i].astype(F32) + came).astype(BF16)
        else:
            ref[to, :] = product_ref[i]
        squares.append(squares_ref[i, 0:1, :])
    if part == 0:
        sums = jnp.concatenate(squares, axis=1) + stripe_sum(came_ref[came_rows:, :].astype(F32))
        if last:
            pad = jnp.zeros((1, cols - rows), F32)
            for i in range(2):
                wide = jnp.concatenate([sums[:, i * rows : (i + 1) * rows], pad], axis=1)
                out_refs[i][rows:, :] = stripe_of(wide)
        else:
            out_refs[0][2 * rows :, :] = stripe_of(sums)


def hop(part, at, last, product, squares, came):
    rows = product.shape[1]
    cols = product.shape[2] // 2
    extra = STRIPE if part == 0 else 0
    came_rows = came.shape[0] - extra
    shapes = [(rows + extra, cols)] * 2 if last else [(2 * rows + extra, cols)]
    return pl.pallas_call(
        functools.partial(hop_kernel, part, came_rows, last),
        out_shape=tuple(jax.ShapeDtypeStruct(s, BF16) for s in shapes),
        grid=(1,),
        in_specs=[
            pl.BlockSpec(
                (pl.Element(2), pl.Element(rows), pl.Element(cols)), lambda i: (at, 0, part * cols)
            ),
            pl.BlockSpec((pl.Element(2), pl.Element(8), pl.Element(rows)), lambda i: (at, 0, 0)),
            pl.BlockSpec(came.shape, lambda i: (0, 0)),
        ],
        out_specs=tuple(pl.BlockSpec(s, lambda i: (0, 0)) for s in shapes),
        compiler_params=PARAMS,
        name="hop",
    )(product, squares, came)


def scaled_sum(product_ref, a_ref, b_ref, inverse, out_ref):
    rows, cols = out_ref.shape
    for i in range(rows // LANES):
        to = slice(i * LANES, (i + 1) * LANES)
        scale = jnp.broadcast_to(inverse[:, to], (LANES, LANES)).T
        for j in range(cols // LANES):
            lane = slice(j * LANES, (j + 1) * LANES)
            total = product_ref[0, to, lane].astype(F32) + a_ref[to, lane].astype(F32)
            out_ref[to, lane] = ((total + b_ref[to, lane].astype(F32)) * scale).astype(BF16)


def finish_keys_kernel(product_ref, squares_ref, k_ref, k2_ref, out_ref, inverse_ref):
    rows = out_ref.shape[0]
    squares = squares_ref[0, 0:1, :]
    squares += stripe_sum(k_ref[rows:, :].astype(F32))[:, :rows]
    squares += stripe_sum(k2_ref[rows:, :].astype(F32))[:, :rows]
    inverse = lax.rsqrt(squares / D + EPS)
    inverse_ref[...] = jnp.broadcast_to(inverse, inverse_ref.shape)
    scaled_sum(product_ref, k_ref, k2_ref, inverse, out_ref)


def finish_values_kernel(product_ref, inverse_ref, v_ref, v2_ref, out_ref):
    scaled_sum(product_ref, v_ref, v2_ref, inverse_ref[0:1, :], out_ref)


def finish(part, product, lane_values, a, b):
    count, rows, cols2 = product.shape
    cols = cols2 // 2
    whole = lambda x: pl.BlockSpec(x.shape, lambda i: (0,) * x.ndim)
    out_shape = [jax.ShapeDtypeStruct((rows, cols), BF16)]
    if part == 0:
        out_shape.append(jax.ShapeDtypeStruct((8, rows), F32))
        lanes = pl.BlockSpec((1, 8, rows), lambda i: (count - 1, 0, 0))
    else:
        lanes = whole(lane_values)
    return pl.pallas_call(
        finish_values_kernel if part else finish_keys_kernel,
        out_shape=tuple(out_shape),
        grid=(1,),
        in_specs=[
            pl.BlockSpec((1, rows, cols), lambda i: (count - 1, 0, part)),
            lanes,
            whole(a),
            whole(b),
        ],
        out_specs=tuple(pl.BlockSpec(x.shape, lambda i: (0, 0)) for x in out_shape),
        compiler_params=PARAMS,
        name="finish",
    )(product, lane_values, a, b)


def local(vis_feats, proj_w, text_embed, dest_group, layout, norm_gain, key_w, value_w):
    n_grp = lax.axis_size("grp")
    n_y = lax.axis_size("y")
    h = lax.axis_index("grp")
    y = lax.axis_index("y")
    c = lax.axis_index("core")
    seq_len, feats = text_embed.shape
    rows = seq_len // (2 * n_y)
    tokens = vis_feats.shape[0]
    run_count = n_grp // 2
    capacity = tokens // run_count
    slot_count = n_grp * capacity
    cols = key_w.shape[1]
    swap = [(0, 1), (1, 0)]
    ring = []
    cross = []
    for i in range(n_y):
        above = 2 * ((i + 1) % n_y)
        below = 2 * ((i - 1) % n_y)
        ring += [(2 * i, above), (2 * i + 1, below + 1)]
        cross += [(2 * i, above + 1), (2 * i + 1, below)]

    group = jnp.full((1,), h, jnp.int32)
    dest = dest_group.reshape(-1, LANES)
    outgoing = source(group, dest, vis_feats, proj_w, slot_count, capacity)
    arrived = lax.all_to_all(
        outgoing.reshape(n_grp, capacity, feats), "grp", 0, 0, tiled=True
    ).reshape(slot_count, feats)

    weight = jnp.concatenate([key_w, value_w], axis=1).astype(F32) * norm_gain[:, None]
    weight = weight.astype(BF16)
    w_other = lax.ppermute(weight, "core", swap)
    blocks = text_embed.reshape(2 * n_y, rows, feats)
    other = lax.ppermute(blocks, "core", swap)

    far = n_y // 2
    offset = [far] + [o for o in range(far - 1, 0, -1) for _ in (0, 1)] + [0]
    second = [0] + [0, 1] * (far - 1) + [0]
    offset = jnp.asarray(offset, jnp.int32)
    second = jnp.asarray(second, jnp.int32)
    up = 2 * ((y + offset) % n_y) + second
    down = 2 * ((y - offset + n_y) % n_y) + 1 - second
    mine = jnp.where(c == 0, up, down)
    slots = slot_positions(group, dest, layout, slot_count, capacity, tokens // LANES)
    text, text_squares = text_products(mine, blocks, other, weight, w_other)
    text = in_hbm(text)

    arrived, text_squares, slots = lax.optimization_barrier((arrived, text_squares, slots))
    arrived_other = lax.ppermute(arrived, "core", swap)
    visual, visual_squares, key_leaf, value_leaf = visual_products(
        mine, *own_products(arrived, weight), arrived_other, w_other, slots, text, text_squares
    )
    flat = ("y", "core")
    streams = [lax.ppermute(key_leaf, flat, ring), lax.ppermute(value_leaf, flat, ring)]
    blocks_of = (mine, slots, visual, visual_squares, text, text_squares)
    merged_blocks = merge(1, 2, *blocks_of)
    ends = []
    for step in range(far - 1):
        last = step == far - 2
        sends = [hop(part, 0, last, *merged_blocks, streams[part]) for part in range(2)]
        for part in range(2):
            streams[part] = lax.ppermute(sends[part][0], flat, ring)
            if last:
                ends.append(lax.ppermute(sends[part][1], flat, cross))
        if not last:
            slots, _, _ = lax.optimization_barrier((slots, sends[0][0], sends[1][0]))
            merged_blocks = merge(
                2 * step + 3, 3 if step == far - 3 else 2, mine, slots, *blocks_of[2:]
            )
    product, squares = merged_blocks
    key_out, inverse = finish(0, product, squares, streams[0], ends[0])
    (value_out,) = finish(1, product, inverse, streams[1], ends[1])
    return (key_out, value_out)


def solution(mesh):
    n_grp, n_sp = mesh.devices.shape
    split = Mesh(mesh.devices.reshape(n_grp, n_sp // 2, 2), ("grp", "y", "core"))
    sp = ("y", "core")
    return jax.shard_map(
        local,
        mesh=split,
        in_specs=(
            P("grp", None),
            P(None, sp),
            P("grp", sp),
            P(),
            P("grp", None),
            P(sp),
            P(sp, None),
            P(sp, None),
        ),
        out_specs=(P(("grp", "y", "core"), None), P(("grp", "y", "core"), None)),
        check_vma=False,
    )
```
